32 devices in a mesh: pairs: 16 (over z, y, core), aux: 2 (over x).
Axes of the slice: x: 2, y: 2, z: 4, core: 2. Of those that a mesh axis runs over, the one named last changes fastest.
Arguments:
- amplitudes: float32 [64, 256, 256], P('pairs'), may hold values from -6 to 6
- factors: float32 [384, 256, 256], P('aux', 'pairs'), may hold values from -0.078125 to 0.078125
- occ_factors: float32 [384, 8, 8], P('aux'), may hold values from -0.5 to 0.5
Outputs:
- resid: float32 [64, 256, 256], P(None, 'pairs', 'aux')
The draws below stay inside these ranges and needn't reach their ends.
All inputs are finite; a program needn't handle non-finite values.
Results may differ from the reference program's by a relative error of at most 0.0001.
Values sent between devices are 32-bit elements; how exact they have to be, the bound alone decides.
No kernel may reach another device: no remote copies, remote signals or barrier semaphores. Data moves between devices by JAX's collectives and lax.ppermute only.
A program may use at most 128 MiB of HBM per device.

```python
import jax
import jax.numpy as jnp
from jax import lax

V = 256
NAUX = 384
OW = 8
PAIRS = 64


def levels(stream_key, shape, shards, least, high):
    factor_of = 1.0
    for position, shards_of in shards:
        heights = jax.random.uniform(jax.random.fold_in(jax.random.fold_in(stream_key, 6), position), (shards_of,), jnp.float32, least / len(shards), high / len(shards))
        factor_of = factor_of * jnp.repeat(jnp.exp(heights), shape[position] // shards_of).reshape((-1,) + (1,) * (len(shape) - 1 - position))
    return factor_of


def gaussian(key, shape, deviation, limit, shards=(), dtype=jnp.bfloat16):
    factor_of = levels(key, shape, shards, -0.22, 0.18) if shards else 1.0
    values = jax.random.normal(key, shape, jnp.float32) * deviation * factor_of
    return jnp.minimum(jnp.maximum(values, -limit), limit).astype(dtype)


def setup_inputs(seed: int = 0) -> dict:
    streams_of = jax.random.split(jax.random.key(seed), 4)
    amplitudes = gaussian(streams_of[0], (PAIRS, V, V), 1.0, 6.0, ((0, 16),), jnp.float32)
    factors = gaussian(streams_of[1], (NAUX, V, V), (V * 20) ** -0.5, 0.078125, ((0, 2), (1, 16)), jnp.float32)
    occ_factors = gaussian(streams_of[2], (NAUX, OW, OW), (OW * 20) ** -0.5, 0.5, ((0, 2),), jnp.float32)
    return dict(amplitudes=amplitudes, factors=factors, occ_factors=occ_factors)


highest = lax.Precision.HIGHEST


def reference(amplitudes, factors, occ_factors):
    def add_factor(running, factor):
        mixed_terms = jnp.einsum('icd,bd->icb', amplitudes, factor, precision=highest)
        return running + jnp.einsum('ac,icb->iab', factor, mixed_terms, precision=highest), None

    particle, unused = lax.scan(add_factor, jnp.zeros(amplitudes.shape, jnp.float32), factors)
    coupling = jnp.einsum('pik,pjl->ijkl', occ_factors, occ_factors, precision=highest).reshape(PAIRS, PAIRS)
    ladder = particle + jnp.einsum('pk,kab->pab', coupling, amplitudes, precision=highest)
    flipped = jnp.swapaxes(ladder, 1, 2).reshape(OW, OW, V, V).transpose(1, 0, 2, 3).reshape(PAIRS, V, V)
    return ladder + flipped
```

```python
import functools

import jax
import jax.numpy as jnp
from jax import lax
from jax.experimental import pallas as pl
from jax.experimental.pallas import tpu as pltpu
from jax.sharding import PartitionSpec as P


highest = lax.Precision.HIGHEST
f32, bf16 = jnp.float32, jnp.bfloat16
MATES = 4
VMEM_BYTES = 60 * 2**20
RUN_SIXTHS = (1, 1, 2, 2)


def halves(value):
    high = value.astype(bf16)
    return high, (value - high.astype(f32)).astype(bf16)


def rows_by_rows(left, right):
    return lax.dot_general(left, right, (((1,), (1,)), ((), ())), preferred_element_type=f32)


def divisor(count, most):
    return max(d for d in range(1, most + 1) if count % d == 0)


def ladder_kernel(started, parts, place, pieces_ref, *refs):
    mates = refs[:MATES]
    before = None if started else refs[MATES]
    refs = refs[MATES + (0 if started else 1) :]
    if parts:
        *outs, total, paired, pair, whole, high, low, mixed_high, mixed_low = refs
    else:
        total, paired, pair, whole, high, low, mixed_high, mixed_low = refs
    layers, planes, count, tall, cols = pieces_ref.shape
    size = total.shape[1]
    block, rows = mates[0].shape[1], mates[0].shape[2]
    layer, mate, plane = place[0], place[1], place[2]

    @pl.when(pl.program_id(0) == 0)
    def _():
        for s in range(count):
            for z in range(layers):
                for c in range(planes):
                    source = pieces_ref[
                        lax.rem(layer - z + layers, layers), lax.rem(plane - c + planes, planes), s
                    ]
                    pair[z * tall : (z + 1) * tall, c * cols : (c + 1) * cols] = source
            h, l = halves(pair[...])
            paired[s] = jnp.concatenate([h, h, l], 1)
        total[...] = jnp.zeros(total.shape, f32) if started else before[...]

    for step in range(layers):
        for m in range(MATES):
            source = lax.rem(layer - step + layers, layers) * MATES + (mate ^ m)
            offset = pl.multiple_of(source * rows, rows)
            whole[:, pl.ds(offset, rows), :] = mates[m][step]
    for p in range(block):
        high[p], low[p] = halves(whole[p])
    h = high[...].reshape(block * size, size)
    l = low[...].reshape(block * size, size)
    stacked = jnp.concatenate([h, l, h], 1)
    for s in range(count):
        mh, ml = halves(rows_by_rows(stacked, paired[s]))
        mixed_high[:, s] = mh.reshape(block, size, size)
        mixed_low[:, s] = ml.reshape(block, size, size)
    group = divisor(count, 3)
    for g in range(0, count, group):
        left, right = [], []
        for p in range(block):
            mh = mixed_high[p, g : g + group].reshape(group * size, size)
            ml = mixed_low[p, g : g + group].reshape(group * size, size)
            left += [mh, ml, mh]
            right += [high[p], high[p], low[p]]
        sums = rows_by_rows(jnp.concatenate(left, 1), jnp.concatenate(right, 1))
        total[g : g + group] += sums.reshape(group, size, size)

    if parts:

        @pl.when(pl.program_id(0) == pl.num_programs(0) - 1)
        def _():
            for n, (first, last, turned) in enumerate(parts):
                for s in range(first, last + turned):
                    value = total[s] if s < last else total[s - last + first].T
                    for step in range(planes):
                        kept = lax.rem(plane + step, planes)
                        chosen = value[:, :cols]
                        for c in range(1, planes):
                            chosen = jnp.where(kept == c, value[:, c * cols : (c + 1) * cols], chosen)
                        outs[n * planes + step][s - first] = chosen


def ladder(place, pieces, factor_mates, before, parts=()):
    layers, planes, count, _, cols = pieces.shape
    _, run, rows, size = factor_mates[0].shape
    block = divisor(run, 4)
    started = before is None
    sums = jax.ShapeDtypeStruct((count, size, size), f32)
    results = [
        jax.ShapeDtypeStruct((last - first + turned, size, cols), f32)
        for first, last, turned in parts
        for _ in range(planes)
    ] or [sums]
    specs = [pl.BlockSpec(result.shape, lambda k, place: (0, 0, 0)) for result in results]
    piece_spec = pl.BlockSpec(pieces.shape, lambda k, place: (0, 0, 0, 0, 0))
    sums_spec = pl.BlockSpec(sums.shape, lambda k, place: (0, 0, 0))
    factor_spec = pl.BlockSpec((layers, block, rows, size), lambda k, place: (0, k, 0, 0))
    flops = 12 * run * count * size**3
    moved = 4 * (run * size * size + 3 * count * size * size)
    kept = [pltpu.VMEM(sums.shape, f32)] if parts else []
    return pl.pallas_call(
        functools.partial(ladder_kernel, started, tuple(parts)),
        grid_spec=pltpu.PrefetchScalarGridSpec(
            num_scalar_prefetch=1,
            grid=(run // block,),
            in_specs=[piece_spec] + [factor_spec] * MATES + ([] if started else [sums_spec]),
            out_specs=specs,
            scratch_shapes=kept
            + [
                pltpu.VMEM((count, size, 3 * size), bf16),
                pltpu.VMEM((size, size), f32),
                pltpu.VMEM((block, size, size), f32),
                pltpu.VMEM((block, size, size), bf16),
                pltpu.VMEM((block, size, size), bf16),
                pltpu.VMEM((block, count, size, size), bf16),
                pltpu.VMEM((block, count, size, size), bf16),
            ],
        ),
        out_shape=results,
        compiler_params=pltpu.CompilerParams(vmem_limit_bytes=VMEM_BYTES),
        cost_estimate=pl.CostEstimate(flops=flops, bytes_accessed=moved, transcendentals=0),
    )(place, pieces, *factor_mates, *([] if started else [before]))


def gather_kernel(where, place, *refs):
    *mates, hole, out, held = refs
    for m in range(MATES):
        held[place[1] ^ m] = mates[m][...]
    for pair, (group, position) in enumerate(where):
        out[pair] = held[group, position] + hole[pair]


def finish(where, place, mates, hole):
    whole = pl.BlockSpec(memory_space=pltpu.VMEM)
    return pl.pallas_call(
        functools.partial(gather_kernel, where),
        in_specs=[pl.BlockSpec(memory_space=pltpu.SMEM)] + [whole] * (MATES + 1),
        out_specs=whole,
        out_shape=jax.ShapeDtypeStruct(hole.shape, f32),
        scratch_shapes=[pltpu.VMEM((MATES,) + mates[0].shape, f32)],
    )(place, *mates, hole)


def shards(amplitudes, factors, occ_factors):
    size = amplitudes.shape[1]
    aux_local, rows, _ = factors.shape
    occupied = occ_factors.shape[1]
    total = occupied * occupied
    planes, devices = lax.axis_size("aux"), lax.axis_size("pairs")
    layers = devices // MATES
    cols = size // planes
    rank, plane = lax.axis_index("pairs"), lax.axis_index("aux")
    layer, mate = rank // MATES, rank % MATES
    place = jnp.stack([layer, mate, plane]).astype(jnp.int32)
    tall = MATES * rows

    def to_layer(value, step):
        def target(d):
            return (d // MATES + step) % layers * MATES + d % MATES

        return lax.ppermute(value, "pairs", [(d, target(d)) for d in range(devices)])

    def to_mate(value, m):
        return lax.ppermute(value, "pairs", [(d, d ^ m) for d in range(devices)])

    def to_plane(value, step):
        return lax.ppermute(value, "aux", [(d, (d + step) % planes) for d in range(planes)])

    off = [(i, j) for i in range(occupied) for j in range(i + 1, occupied)]
    n_off, n_diag = len(off) // MATES, occupied // MATES
    groups = [
        off[g * n_off : (g + 1) * n_off] + [(i, i) for i in range(g * n_diag, (g + 1) * n_diag)]
        for g in range(MATES)
    ]
    count = n_off + n_diag

    straight = lax.dynamic_slice_in_dim(amplitudes, plane * cols, cols, 2)
    turned = jnp.swapaxes(lax.dynamic_slice_in_dim(amplitudes, plane * cols, cols, 1), 1, 2)
    both = lax.all_to_all(
        jnp.stack([straight, turned]), "pairs", split_axis=2, concat_axis=1, tiled=True
    )
    both = both.reshape(2, occupied, occupied, rows, cols)
    own_sums = (both[0] + both[1].swapaxes(0, 1)).reshape(total, rows, cols)

    chosen = jnp.stack([own_sums[j * occupied + i] for group in groups for i, j in group])
    chosen = chosen.reshape(MATES, count, rows, cols)
    piece = jnp.zeros((count, tall, cols), f32)
    for m in range(MATES):
        sending = lax.dynamic_index_in_dim(chosen, mate ^ m, 0, keepdims=False)
        got = to_mate(sending, m) if m else sending
        piece = lax.dynamic_update_slice(piece, got, (0, (mate ^ m) * rows, 0))
    pieces = []
    for step in range(layers):
        slab = to_layer(piece, step) if step else piece
        for across in range(planes):
            pieces.append(to_plane(slab, across) if across else slab)
    pieces = jnp.stack(pieces).reshape(layers, planes, count, tall, cols)

    share = aux_local // layers
    sizes = [share // 6 * n for n in RUN_SIXTHS] if share % 6 == 0 else [share]
    runs = len(sizes)
    by_layer = factors.reshape(layers, share, rows, size)
    mates_of = []
    for k in range(runs):
        source = by_layer[:, sum(sizes[:k]) : sum(sizes[: k + 1])]
        stack = [lax.dynamic_index_in_dim(source, layer, 0, keepdims=False)]
        for step in range(1, layers):
            sending = lax.dynamic_index_in_dim(source, (layer + step) % layers, 0, keepdims=False)
            stack.append(to_layer(sending, step))
        own = jnp.stack(stack)
        across = to_mate(own, 2)
        mates_of.append([own, to_mate(own, 1), across, to_mate(across, 1)])

    coupling = jnp.einsum("pik,pjl->ijkl", occ_factors, occ_factors, precision=highest)
    coupling = coupling.reshape(total, total)
    coupling = coupling + sum(to_plane(coupling, step) for step in range(1, planes))
    hole = jnp.einsum("pk,kab->pab", coupling, own_sums, precision=highest)

    each = count // divisor(count, 3)
    parts, where = [], {}
    filled = 0
    for first in range(0, count, each):
        members = range(first, first + each)
        turned = sum(s < n_off for s in members)
        parts.append((first, first + each, turned))
        for g in range(MATES):
            for n, s in enumerate(members):
                i, j = groups[g][s]
                where[i * occupied + j] = (g, filled + n)
                if s < n_off:
                    where[j * occupied + i] = (g, filled + each + n)
        filled += each + turned

    result = None
    for k in range(runs):
        if k == 1:
            place, hole = lax.optimization_barrier((place, hole))
        outs = ladder(place, pieces, mates_of[k], result, parts if k == runs - 1 else ())
        result = outs[0]
    done = []
    for part in range(len(parts)):
        mine, *others = outs[part * planes : (part + 1) * planes]
        got = [to_plane(other, step + 1) for step, other in enumerate(others)]
        mine = sum(got, mine)
        terms = [
            lax.dynamic_slice_in_dim(mine, (layer + step) % layers * tall, tall, 1)
            for step in range(layers)
        ]
        terms = [to_layer(t, step) if step else t for step, t in enumerate(terms)]
        done.append(terms)
    done = lax.optimization_barrier(done)
    summed = jnp.concatenate([sum(terms) for terms in done], 0)
    mates = []
    for m in range(MATES):
        sending = lax.dynamic_slice_in_dim(summed, (mate ^ m) * rows, rows, 1)
        mates.append(to_mate(sending, m) if m else sending)
    return finish([where[p] for p in range(total)], place, mates, hole)


def solution(mesh):
    placed = (P("pairs", None, None), P("aux", "pairs", None), P("aux", None, None))
    return jax.shard_map(
        shards, mesh=mesh, in_specs=placed, out_specs=P(None, "pairs", "aux"), check_vma=False
    )
```
